32 devices in a mesh: dp: 4 (over y, x), seq: 4 (over z), tp: 2 (over core).
Axes of the slice: x: 2, y: 2, z: 4, core: 2. Of those that a mesh axis runs over, the one named last changes fastest.
Arguments:
- queries: bfloat16 [4, 2048, 5120], P('dp', 'seq', 'tp'), may hold values from -200 to 200
- keys: bfloat16 [4, 512, 5120], P('dp', None, 'tp'), may hold values from -6 to 6
- values: bfloat16 [4, 512, 5120], P('dp', None, 'tp'), may hold values from -6 to 6
- grad_attention: bfloat16 [4, 2048, 5120], P('dp', 'seq', 'tp'), may hold values from -48 to 48
- normed: bfloat16 [4, 512, 4096], P('dp', None, 'seq'), may hold values from -6 to 6
- norm_scale: float32 [4, 512], P('dp'), may hold values from 0.3 to 3
- norm_gain: float32 [4096], P('seq'), may hold values from 0.1 to 1.9
- key_weight: bfloat16 [4096, 5120], P('seq', 'tp'), may hold values from -0.078125 to 0.078125
- value_weight: bfloat16 [4096, 5120], P('seq', 'tp'), may hold values from -0.078125 to 0.078125
- key_down: bfloat16 [4096, 32], P('seq'), may hold values from -0.09375 to 0.09375
- key_up: bfloat16 [32, 5120], P(None, 'tp'), may hold values from -0.078125 to 0.078125
- value_down: bfloat16 [4096, 32], P('seq'), may hold values from -0.09375 to 0.09375
- value_up: bfloat16 [32, 5120], P(None, 'tp'), may hold values from -0.078125 to 0.078125
- out_weight: bfloat16 [10240, 4096], P('tp', 'seq'), may hold values from -0.09375 to 0.09375
Outputs:
- grad_queries: bfloat16 [4, 2048, 5120], P('dp', 'seq', 'tp')
- grad_text: bfloat16 [4, 512, 4096], P('dp', None, 'seq')
- grad_hidden: bfloat16 [4, 512, 10240], P('dp', 'seq', 'tp')
- grad_key_down: float32 [4096, 32], P('seq')
- grad_key_up: float32 [32, 5120], P(None, 'tp')
- grad_value_down: float32 [4096, 32], P('seq')
- grad_value_up: float32 [32, 5120], P(None, 'tp')
The draws below stay inside these ranges and needn't reach their ends.
All inputs are finite; a program needn't handle non-finite values.
Results may differ from the reference program's by a relative error of at most 0.03.
Values may be sent and summed in bfloat16 or wider, within the bound.
A program may use at most 192 MiB of HBM per device.

```python
import math
import jax
import jax.numpy as jnp
from jax import lax

D = 5120
H = 40
HD = 128
DT = 4096
FF = 10240
R = 32
LTXT = 512
IMG_DEV = 512
IMG = 2048
PROMPTS = 4
N_SEQ = 4


def key_table(key):
    table = jnp.clip(jax.random.normal(jax.random.fold_in(key, 101), (PROMPTS, LTXT, D), jnp.float32), -5.0, 5.0)
    return table


def draw_keys(key, part):
    return key_table(key).astype(jnp.bfloat16)


def draw_queries(key, part):
    table = jnp.clip(jax.random.normal(jax.random.fold_in(key, 103), (PROMPTS, IMG, D), jnp.float32), -5.0, 5.0)
    return table.astype(jnp.bfloat16)


def levels(own_key, dims, shards, low, high):
    gain, own = 1.0, jax.random.fold_in(own_key, 6)
    for position, parts in shards:
        steps = jnp.exp(jax.random.uniform(jax.random.fold_in(own, position), (parts,), jnp.float32, low / len(shards), high / len(shards)))
        gain = gain * jnp.repeat(steps, dims[position] // parts).reshape([-1 if axis == position else 1 for axis in range(len(dims))])
    return gain


def gaussian(key, dims, deviation, most, pieces=(), kind=jnp.bfloat16):
    level = levels(key, dims, pieces, -0.22, 0.18) if pieces else 1.0
    drawn = jax.random.normal(key, dims, jnp.float32) * deviation * level
    return jnp.minimum(jnp.maximum(drawn, -most), most).astype(kind)


def setup_inputs(seed: int = 0) -> dict:
    streams_of = jax.random.split(jax.random.key(seed), 15)
    queries = draw_queries(jax.random.fold_in(streams_of[14], 71), 0)
    keys = draw_keys(jax.random.fold_in(streams_of[14], 71), 0)
    values = gaussian(streams_of[2], (PROMPTS, LTXT, D), 1.0, 6.0, ((0, 4), (2, 2)))
    grad_attention = gaussian(streams_of[3], (PROMPTS, IMG, D), 8.0, 48.0, ((0, 4), (1, 4), (2, 2)))
    normed = gaussian(streams_of[4], (PROMPTS, LTXT, DT), 1.0, 6.0, ((0, 4), (2, 4)))
    norm_scale = jnp.clip(jnp.exp(math.log(3.0) - 2.3025851 * jax.random.uniform(streams_of[5], (PROMPTS, LTXT), jnp.float32) ** levels(streams_of[5], (PROMPTS, LTXT), ((0, 4),), -0.2, 0.2)), 0.3, 3.0)
    norm_gain = jnp.clip(1.0 + 0.18 * jax.random.normal(streams_of[6], (DT,), jnp.float32), 0.1, 1.9)
    key_weight = gaussian(streams_of[7], (DT, D), D ** -0.5, 0.078125, ((0, 4), (1, 2)))
    value_weight = gaussian(streams_of[8], (DT, D), D ** -0.5, 0.078125, ((0, 4), (1, 2)))
    key_down = gaussian(streams_of[9], (DT, R), DT ** -0.5, 0.09375, ((0, 4),))
    key_up = gaussian(streams_of[10], (R, D), D ** -0.5, 0.078125, ((1, 2),))
    value_down = gaussian(streams_of[11], (DT, R), DT ** -0.5, 0.09375, ((0, 4),))
    value_up = gaussian(streams_of[12], (R, D), D ** -0.5, 0.078125, ((1, 2),))
    out_weight = gaussian(streams_of[13], (FF, DT), DT ** -0.5, 0.09375, ((0, 2), (1, 4)))
    return dict(queries=queries, keys=keys, values=values, grad_attention=grad_attention, normed=normed, norm_scale=norm_scale, norm_gain=norm_gain, key_weight=key_weight, value_weight=value_weight, key_down=key_down, key_up=key_up, value_down=value_down, value_up=value_up, out_weight=out_weight)


def settle(partial_values):
    return lax.optimization_barrier(partial_values.astype(jnp.bfloat16)).astype(jnp.float32)


def head_grads(operands):
    query_rows, key_rows, value_rows, grad_rows = operands
    factor = HD ** -0.5
    scores = jnp.dot(query_rows, key_rows.T, preferred_element_type=jnp.float32) * factor
    weights = jnp.exp(scores - jnp.max(scores, axis=1, keepdims=True))
    probability = weights / jnp.sum(weights, axis=1, keepdims=True)
    weights_low = probability.astype(jnp.bfloat16)
    grad_probs = jnp.dot(grad_rows, value_rows.T, preferred_element_type=jnp.float32)
    grad_scores = probability * (grad_probs - jnp.sum(probability * grad_probs, axis=1, keepdims=True))
    grad_low = grad_scores.astype(jnp.bfloat16)
    grad_query = (jnp.dot(grad_low, key_rows, preferred_element_type=jnp.float32) * factor).astype(jnp.bfloat16)
    low_blocks = grad_low.reshape(N_SEQ, IMG_DEV, LTXT).astype(jnp.float32)
    weight_blocks = weights_low.reshape(N_SEQ, IMG_DEV, LTXT).astype(jnp.float32)
    query_blocks = query_rows.reshape(N_SEQ, IMG_DEV, HD).astype(jnp.float32)
    grad_blocks = grad_rows.reshape(N_SEQ, IMG_DEV, HD).astype(jnp.float32)
    grad_key = jnp.sum(settle(jnp.einsum("sij,sid->sjd", low_blocks, query_blocks) * factor), axis=0)
    grad_value = jnp.sum(settle(jnp.einsum("sij,sid->sjd", weight_blocks, grad_blocks)), axis=0)
    return grad_query, grad_key, grad_value


def block_latent(context, down_factor):
    slab_width = DT // N_SEQ
    context_blocks = context.reshape(LTXT, N_SEQ, slab_width).transpose(1, 0, 2).astype(jnp.float32)
    down_blocks = down_factor.reshape(N_SEQ, slab_width, R).astype(jnp.float32)
    return jnp.sum(settle(jnp.einsum("slc,scr->slr", context_blocks, down_blocks)), axis=0).astype(jnp.bfloat16)


def reference(queries, keys, values, grad_attention, normed, norm_scale, norm_gain, key_weight, value_weight, key_down, key_up, value_down, value_up, out_weight):
    slab_width = DT // N_SEQ
    query_list, text_list, hidden_list = [], [], []
    key_down_sum = jnp.zeros((DT, R), jnp.float32)
    value_down_sum = jnp.zeros((DT, R), jnp.float32)
    key_up_sum = jnp.zeros((R, D), jnp.float32)
    value_up_sum = jnp.zeros((R, D), jnp.float32)
    for prompt in range(PROMPTS):
        query_heads = queries[prompt].reshape(IMG, H, HD).transpose(1, 0, 2)
        key_heads = keys[prompt].reshape(LTXT, H, HD).transpose(1, 0, 2)
        value_heads = values[prompt].reshape(LTXT, H, HD).transpose(1, 0, 2)
        grad_heads = grad_attention[prompt].reshape(IMG, H, HD).transpose(1, 0, 2)
        grad_query, grad_key, grad_value = lax.map(head_grads, (query_heads, key_heads, value_heads, grad_heads))
        query_list.append(grad_query.transpose(1, 0, 2).reshape(IMG, D))
        key_grad = grad_key.transpose(1, 0, 2).reshape(LTXT, D).astype(jnp.bfloat16)
        value_grad = grad_value.transpose(1, 0, 2).reshape(LTXT, D).astype(jnp.bfloat16)
        context = (normed[prompt].astype(jnp.float32) * norm_gain).astype(jnp.bfloat16)
        key_latent = block_latent(context, key_down)
        value_latent = block_latent(context, value_down)
        key_back = jnp.dot(key_grad, key_up.T, preferred_element_type=jnp.float32).astype(jnp.bfloat16)
        value_back = jnp.dot(value_grad, value_up.T, preferred_element_type=jnp.float32).astype(jnp.bfloat16)
        grad_context = jnp.dot(key_grad, key_weight.T, preferred_element_type=jnp.float32)
        grad_context = grad_context + jnp.dot(value_grad, value_weight.T, preferred_element_type=jnp.float32)
        grad_context = grad_context + jnp.dot(key_back, key_down.T, preferred_element_type=jnp.float32)
        grad_context = grad_context + jnp.dot(value_back, value_down.T, preferred_element_type=jnp.float32)
        text_rows = normed[prompt].astype(jnp.float32)
        scaled = norm_gain * grad_context
        token_sum = jnp.sum(text_rows * scaled, axis=1, keepdims=True)
        grad_text = (norm_scale[prompt][:, None] * (scaled - text_rows * token_sum / DT)).astype(jnp.bfloat16)
        text_list.append(grad_text)
        hidden = jnp.zeros((LTXT, FF), jnp.float32)
        for block_index in range(N_SEQ):
            offset = block_index * slab_width
            hidden = hidden + settle(jnp.dot(grad_text[:, offset:offset + slab_width], out_weight[:, offset:offset + slab_width].T, preferred_element_type=jnp.float32))
        hidden_list.append(hidden.astype(jnp.bfloat16))
        key_down_sum = key_down_sum + jnp.dot(context.T, key_back, preferred_element_type=jnp.float32)
        value_down_sum = value_down_sum + jnp.dot(context.T, value_back, preferred_element_type=jnp.float32)
        key_up_sum = key_up_sum + jnp.dot(key_latent.T, key_grad, preferred_element_type=jnp.float32)
        value_up_sum = value_up_sum + jnp.dot(value_latent.T, value_grad, preferred_element_type=jnp.float32)
    return (jnp.stack(query_list), jnp.stack(text_list), jnp.stack(hidden_list), key_down_sum / PROMPTS, key_up_sum / PROMPTS, value_down_sum / PROMPTS, value_up_sum / PROMPTS)
```

```python
import functools

import jax
import jax.numpy as jnp
from jax import lax
from jax.experimental import pallas as pl
from jax.experimental.pallas import tpu as pltpu
from jax.sharding import PartitionSpec as P

HD = 128
DT = 4096
MESH = pl.DeviceIdType.MESH


def contract_last(left_side, right_side):
    return lax.dot_general(
        left_side, right_side, (((1,), (1,)), ((), ())), preferred_element_type=jnp.float32
    )


def contract_first(left_side, right_side):
    return lax.dot_general(
        left_side, right_side, (((0,), (0,)), ((), ())), preferred_element_type=jnp.float32
    )


def dot(left_side, right_side, left_dim, right_dim):
    return lax.dot_general(
        left_side,
        right_side,
        (((left_dim,), (right_dim,)), ((), ())),
        preferred_element_type=jnp.float32,
    )


def attention_kernel(
    n,
    heads,
    lag,
    queries,
    keys,
    values,
    grads,
    key_weight,
    value_weight,
    key_up,
    value_up,
    grad_query,
    key_grad,
    value_grad,
    context,
    key_project,
    value_project,
    part,
    up_in,
    up_out,
    down_in,
    down_out,
    total,
    key_total,
    value_total,
    up_send,
    up_recv,
    down_send,
    down_recv,
):
    step = pl.program_id(0)
    me = lax.axis_index("seq")
    factor = HD ** (-0.5)
    has_low = me > 0
    has_high = me < n - 1

    def up_copy(chunk, source):
        return pltpu.make_async_remote_copy(
            src_ref=source.at[chunk],
            dst_ref=up_in.at[chunk],
            send_sem=up_send.at[chunk],
            recv_sem=up_recv.at[chunk],
            device_id={"seq": lax.rem(me + 1, n)},
            device_id_type=MESH,
        )

    def down_copy(chunk, source):
        return pltpu.make_async_remote_copy(
            src_ref=source.at[chunk],
            dst_ref=down_in.at[chunk],
            send_sem=down_send.at[chunk],
            recv_sem=down_recv.at[chunk],
            device_id={"seq": lax.rem(me + n - 1, n)},
            device_id_type=MESH,
        )

    @pl.when(step == 0)
    def _():
        barrier = pltpu.get_barrier_semaphore()

        @pl.when(has_low)
        def _():
            pl.semaphore_signal(
                barrier,
                inc=1,
                device_id={"seq": lax.rem(me + n - 1, n)},
                device_id_type=MESH,
            )

        @pl.when(has_high)
        def _():
            pl.semaphore_signal(
                barrier, inc=1, device_id={"seq": lax.rem(me + 1, n)}, device_id_type=MESH
            )

        total[...] = jnp.zeros_like(total)
        key_total[...] = jnp.zeros_like(key_total)
        value_total[...] = jnp.zeros_like(value_total)

        pl.semaphore_wait(barrier, has_low.astype(jnp.int32) + has_high.astype(jnp.int32))

    @pl.when(step < heads)
    def _():
        query, key, value, grad = queries[...], keys[...], values[...], grads[...]
        scores = dot(key, query, 1, 1) * factor
        weights = jnp.exp(scores - jnp.max(scores, axis=0, keepdims=True))
        probability = weights * (1.0 / jnp.sum(weights, axis=0, keepdims=True))
        part[step, :, HD:] = dot(probability.astype(jnp.bfloat16), grad, 1, 0).astype(jnp.bfloat16)
        grad_probs = dot(value, grad, 1, 1)
        grad_scores = probability * (
            grad_probs - jnp.sum(probability * grad_probs, axis=0, keepdims=True)
        )
        grad_low = grad_scores.astype(jnp.bfloat16)
        part[step, :, :HD] = (dot(grad_low, query, 1, 0) * factor).astype(jnp.bfloat16)
        grad_query[...] = (dot(grad_low, key, 0, 0) * factor).astype(jnp.bfloat16)

    up_chunk = step - me
    up_live = jnp.logical_and(up_chunk >= 0, up_chunk < heads)

    @pl.when(jnp.logical_and(up_live, has_low))
    def _():
        up_copy(up_chunk, up_out).wait_recv()

        @pl.when(has_high)
        def _():
            up_out[up_chunk] = up_in[up_chunk] + part[up_chunk]
            up_copy(up_chunk, up_out).start()

    @pl.when(jnp.logical_and(up_live, me == 0))
    def _():
        up_copy(up_chunk, part).start()
        up_in[up_chunk] = jnp.zeros(up_in.shape[1:], up_in.dtype)

    down_chunk = step - (n - 1 - me)
    down_live = jnp.logical_and(down_chunk >= 0, down_chunk < heads)

    @pl.when(jnp.logical_and(down_live, has_high))
    def _():
        down_copy(down_chunk, down_out).wait_recv()

        @pl.when(has_low)
        def _():
            down_out[down_chunk] = down_in[down_chunk] + part[down_chunk]
            down_copy(down_chunk, down_out).start()

    @pl.when(jnp.logical_and(down_live, me == n - 1))
    def _():
        down_copy(down_chunk, part).start()
        down_in[down_chunk] = jnp.zeros(down_in.shape[1:], down_in.dtype)

    @pl.when(step >= lag)
    def _():
        chunk = step - lag

        @pl.when(has_high)
        def _():
            up_copy(chunk, up_out).wait_send()

        @pl.when(has_low)
        def _():
            down_copy(chunk, down_out).wait_send()

        both = (
            up_in[chunk].astype(jnp.float32)
            + part[chunk].astype(jnp.float32)
            + down_in[chunk].astype(jnp.float32)
        ).astype(jnp.bfloat16)
        key_grad[...] = both[:, :HD]
        value_grad[...] = both[:, HD:]
        slab = jnp.concatenate([key_weight[...], value_weight[...]], axis=1)
        total[...] += dot(both, slab, 1, 1)
        key_total[...] += dot(both[:, :HD], key_up[...], 1, 1)
        value_total[...] += dot(both[:, HD:], value_up[...], 1, 1)

    @pl.when(step == heads + lag - 1)
    def _():
        context[...] = total[...].astype(jnp.bfloat16)
        key_project[...] = key_total[...].astype(jnp.bfloat16)
        value_project[...] = value_total[...].astype(jnp.bfloat16)


def attention_grads(
    queries, keys, values, grad_attention, key_weight, value_weight, key_up, value_up
):
    rows, columns = queries.shape
    length = keys.shape[0]
    features = key_weight.shape[0]
    rank = key_up.shape[0]
    heads = columns // HD
    n = lax.axis_size("seq")
    lag = n + 1

    def early(height):
        return pl.BlockSpec((height, HD), lambda step: (0, jnp.minimum(step, heads - 1)))

    def late(height):
        return pl.BlockSpec((height, HD), lambda step: (0, jnp.maximum(step - lag, 0)))

    def fixed(height, width):
        return pl.BlockSpec((height, width), lambda step: (0, 0))

    buffer = pltpu.VMEM((heads, length, 2 * HD), jnp.bfloat16)
    semaphores = pltpu.SemaphoreType.DMA((heads,))
    return pl.pallas_call(
        functools.partial(attention_kernel, n, heads, lag),
        grid=(heads + lag,),
        out_shape=(
            jax.ShapeDtypeStruct((rows, columns), jnp.bfloat16),
            jax.ShapeDtypeStruct((length, columns), jnp.bfloat16),
            jax.ShapeDtypeStruct((length, columns), jnp.bfloat16),
            jax.ShapeDtypeStruct((length, features), jnp.bfloat16),
            jax.ShapeDtypeStruct((length, rank), jnp.bfloat16),
            jax.ShapeDtypeStruct((length, rank), jnp.bfloat16),
        ),
        in_specs=[
            early(rows),
            early(length),
            early(length),
            early(rows),
            late(features),
            late(features),
            late(rank),
            late(rank),
        ],
        out_specs=(
            early(rows),
            late(length),
            late(length),
            fixed(length, features),
            fixed(length, rank),
            fixed(length, rank),
        ),
        scratch_shapes=[buffer] * 5
        + [
            pltpu.VMEM((length, features), jnp.float32),
            pltpu.VMEM((length, rank), jnp.float32),
            pltpu.VMEM((length, rank), jnp.float32),
        ]
        + [semaphores] * 4,
        compiler_params=pltpu.CompilerParams(
            collective_id=0, has_side_effects=True, vmem_limit_bytes=50 * 1024 * 1024
        ),
        cost_estimate=pl.CostEstimate(
            flops=14 * rows * length * columns,
            bytes_accessed=12 * rows * columns,
            transcendentals=rows * length * heads,
        ),
        name="attention",
    )(queries, keys, values, grad_attention, key_weight, value_weight, key_up, value_up)


def norm_backward(
    context_base, key_back, value_back, text_rows, scale_rows, norm_gain, key_down, value_down
):
    grad_context = (
        context_base + contract_last(key_back, key_down) + contract_last(value_back, value_down)
    )
    text_values = text_rows.astype(jnp.float32)
    scaled = norm_gain * grad_context
    local_sum = jnp.sum(text_values * scaled, axis=1)
    token_sum = lax.psum(local_sum, "seq")
    return (scale_rows[:, None] * (scaled - text_values * (token_sum / DT)[:, None])).astype(
        jnp.bfloat16
    )


def shards(
    queries,
    keys,
    values,
    grad_attention,
    normed,
    norm_scale,
    norm_gain,
    key_weight,
    value_weight,
    key_down,
    key_up,
    value_down,
    value_up,
    out_weight,
):
    context = (normed[0].astype(jnp.float32) * norm_gain).astype(jnp.bfloat16)
    latent_part = jnp.concatenate(
        [
            jnp.dot(context, key_down, preferred_element_type=jnp.float32),
            jnp.dot(context, value_down, preferred_element_type=jnp.float32),
        ],
        axis=1,
    )
    latent = lax.psum(latent_part.astype(jnp.bfloat16), "seq")
    grad_query, key_grad, value_grad, context_part, key_project, value_project = attention_grads(
        queries[0],
        keys[0],
        values[0],
        grad_attention[0],
        key_weight,
        value_weight,
        key_up,
        value_up,
    )
    context_base, key_total, value_total = (
        lax.psum(context_part, "tp").astype(jnp.float32),
        lax.psum(key_project, "tp").astype(jnp.float32),
        lax.psum(value_project, "tp").astype(jnp.float32),
    )
    key_back = key_total.astype(jnp.bfloat16)
    value_back = value_total.astype(jnp.bfloat16)
    grad_text = norm_backward(
        context_base,
        key_back,
        value_back,
        normed[0],
        norm_scale[0],
        norm_gain,
        key_down,
        value_down,
    )
    prompt_count = lax.axis_size("dp")
    down_key = contract_first(context, key_back)
    down_value = contract_first(context, value_back)
    rank = key_down.shape[1]
    block = key_grad.shape[0] // lax.axis_size("seq")
    start = lax.axis_index("seq") * block
    latent_block = lax.dynamic_slice_in_dim(latent, start, block, 0)
    up_key = contract_first(
        latent_block[:, :rank], lax.dynamic_slice_in_dim(key_grad, start, block, 0)
    )
    up_value = contract_first(
        latent_block[:, rank:], lax.dynamic_slice_in_dim(value_grad, start, block, 0)
    )
    down_key, down_value = (
        lax.psum(down_key.astype(jnp.bfloat16), "dp").astype(jnp.float32),
        lax.psum(down_value.astype(jnp.bfloat16), "dp").astype(jnp.float32),
    )
    up_key, up_value = (
        lax.psum(up_key.astype(jnp.bfloat16), ("dp", "seq")).astype(jnp.float32),
        lax.psum(up_value.astype(jnp.bfloat16), ("dp", "seq")).astype(jnp.float32),
    )
    grad_hidden = lax.psum_scatter(
        contract_last(grad_text, out_weight).astype(jnp.bfloat16),
        "seq",
        scatter_dimension=0,
        tiled=True,
    )
    return (
        grad_query[None],
        grad_text[None],
        grad_hidden[None],
        down_key / prompt_count,
        up_key / prompt_count,
        down_value / prompt_count,
        up_value / prompt_count,
    )


def solution(mesh):
    return jax.shard_map(
        shards,
        mesh=mesh,
        in_specs=(
            P("dp", "seq", "tp"),
            P("dp", None, "tp"),
            P("dp", None, "tp"),
            P("dp", "seq", "tp"),
            P("dp", None, "seq"),
            P("dp", None),
            P("seq"),
            P("seq", "tp"),
            P("seq", "tp"),
            P("seq", None),
            P(None, "tp"),
            P("seq", None),
            P(None, "tp"),
            P("tp", "seq"),
        ),
        out_specs=(
            P("dp", "seq", "tp"),
            P("dp", None, "seq"),
            P("dp", "seq", "tp"),
            P("seq", None),
            P(None, "tp"),
            P("seq", None),
            P(None, "tp"),
        ),
        check_vma=False,
    )
```

```python
import functools

import jax
import jax.numpy as jnp
from jax import lax
from jax.experimental import pallas as pl
from jax.experimental.pallas import tpu as pltpu
from jax.sharding import PartitionSpec as P

HD = 128
MESH = pl.DeviceIdType.MESH


def dot(left_side, right_side, left_dim, right_dim):
    return lax.dot_general(
        left_side,
        right_side,
        (((left_dim,), (right_dim,)), ((), ())),
        preferred_element_type=jnp.float32,
    )


def attention_kernel(
    n,
    heads,
    lag,
    queries,
    keys,
    values,
    grads,
    key_weight,
    value_weight,
    key_up,
    value_up,
    grad_query,
    key_grad,
    value_grad,
    context,
    project,
    part,
    up_in,
    up_out,
    down_in,
    down_out,
    total,
    key_total,
    value_total,
    up_send,
    up_recv,
    down_send,
    down_recv,
):
    step = pl.program_id(0)
    me = lax.axis_index("seq")
    factor = HD ** (-0.5)
    has_low = me > 0
    has_high = me < n - 1

    def up_copy(chunk, source):
        return pltpu.make_async_remote_copy(
            src_ref=source.at[chunk],
            dst_ref=up_in.at[chunk],
            send_sem=up_send.at[chunk],
            recv_sem=up_recv.at[chunk],
            device_id={"seq": lax.rem(me + 1, n)},
            device_id_type=MESH,
        )

    def down_copy(chunk, source):
        return pltpu.make_async_remote_copy(
            src_ref=source.at[chunk],
            dst_ref=down_in.at[chunk],
            send_sem=down_send.at[chunk],
            recv_sem=down_recv.at[chunk],
            device_id={"seq": lax.rem(me + n - 1, n)},
            device_id_type=MESH,
        )

    @pl.when(step == 0)
    def _():
        barrier = pltpu.get_barrier_semaphore()

        @pl.when(has_low)
        def _():
            pl.semaphore_signal(
                barrier,
                inc=1,
                device_id={"seq": lax.rem(me + n - 1, n)},
                device_id_type=MESH,
            )

        @pl.when(has_high)
        def _():
            pl.semaphore_signal(
                barrier, inc=1, device_id={"seq": lax.rem(me + 1, n)}, device_id_type=MESH
            )

        total[...] = jnp.zeros_like(total)
        key_total[...] = jnp.zeros_like(key_total)
        value_total[...] = jnp.zeros_like(value_total)

        pl.semaphore_wait(barrier, has_low.astype(jnp.int32) + has_high.astype(jnp.int32))

    @pl.when(step < heads)
    def _():
        query, key, value, grad = queries[...], keys[...], values[...], grads[...]
        scores = dot(key, query, 1, 1) * factor
        weights = jnp.exp(scores - jnp.max(scores, axis=0, keepdims=True))
        probability = weights * (1.0 / jnp.sum(weights, axis=0, keepdims=True))
        part[step, :, HD:] = dot(probability.astype(jnp.bfloat16), grad, 1, 0).astype(jnp.bfloat16)
        grad_probs = dot(value, grad, 1, 1)
        grad_scores = probability * (
            grad_probs - jnp.sum(probability * grad_probs, axis=0, keepdims=True)
        )
        grad_low = grad_scores.astype(jnp.bfloat16)
        part[step, :, :HD] = (dot(grad_low, query, 1, 0) * factor).astype(jnp.bfloat16)
        grad_query[...] = (dot(grad_low, key, 0, 0) * factor).astype(jnp.bfloat16)

    up_chunk = step - me
    up_live = jnp.logical_and(up_chunk >= 0, up_chunk < heads)

    @pl.when(jnp.logical_and(up_live, has_low))
    def _():
        up_copy(up_chunk, up_out).wait_recv()

        @pl.when(has_high)
        def _():
            up_out[up_chunk] = up_in[up_chunk] + part[up_chunk]
            up_copy(up_chunk, up_out).start()

    @pl.when(jnp.logical_and(up_live, me == 0))
    def _():
        up_copy(up_chunk, part).start()
        up_in[up_chunk] = jnp.zeros(up_in.shape[1:], up_in.dtype)

    down_chunk = step - (n - 1 - me)
    down_live = jnp.logical_and(down_chunk >= 0, down_chunk < heads)

    @pl.when(jnp.logical_and(down_live, has_high))
    def _():
        down_copy(down_chunk, down_out).wait_recv()

        @pl.when(has_low)
        def _():
            down_out[down_chunk] = down_in[down_chunk] + part[down_chunk]
            down_copy(down_chunk, down_out).start()

    @pl.when(jnp.logical_and(down_live, me == n - 1))
    def _():
        down_copy(down_chunk, part).start()
        down_in[down_chunk] = jnp.zeros(down_in.shape[1:], down_in.dtype)

    @pl.when(step >= lag)
    def _():
        chunk = step - lag

        @pl.when(has_high)
        def _():
            up_copy(chunk, up_out).wait_send()

        @pl.when(has_low)
        def _():
            down_copy(chunk, down_out).wait_send()

        both = (
            up_in[chunk].astype(jnp.float32)
            + part[chunk].astype(jnp.float32)
            + down_in[chunk].astype(jnp.float32)
        ).astype(jnp.bfloat16)
        key_grad[...] = both[:, :HD]
        value_grad[...] = both[:, HD:]
        slab = jnp.concatenate([key_weight[...], value_weight[...]], axis=1)
        total[...] += dot(both, slab, 1, 1)
        key_total[...] += dot(both[:, :HD], key_up[...], 1, 1)
        value_total[...] += dot(both[:, HD:], value_up[...], 1, 1)

    @pl.when(step == heads + lag - 1)
    def _():
        context[...] = total[...].astype(jnp.bfloat16)
        project[...] = jnp.concatenate([key_total[...], value_total[...]], axis=1).astype(
            jnp.bfloat16
        )


def attention_grads(
    queries, keys, values, grad_attention, key_weight, value_weight, key_up, value_up
):
    rows, columns = queries.shape
    length = keys.shape[0]
    features = key_weight.shape[0]
    rank = key_up.shape[0]
    heads = columns // HD
    n = lax.axis_size("seq")
    lag = n + 1

    def early(height):
        return pl.BlockSpec((height, HD), lambda step: (0, jnp.minimum(step, heads - 1)))

    def late(height):
        return pl.BlockSpec((height, HD), lambda step: (0, jnp.maximum(step - lag, 0)))

    def fixed(height, width):
        return pl.BlockSpec((height, width), lambda step: (0, 0))

    buffer = pltpu.VMEM((heads, length, 2 * HD), jnp.bfloat16)
    semaphores = pltpu.SemaphoreType.DMA((heads,))
    return pl.pallas_call(
        functools.partial(attention_kernel, n, heads, lag),
        grid=(heads + lag,),
        out_shape=(
            jax.ShapeDtypeStruct((rows, columns), jnp.bfloat16),
            jax.ShapeDtypeStruct((length, columns), jnp.bfloat16),
            jax.ShapeDtypeStruct((length, columns), jnp.bfloat16),
            jax.ShapeDtypeStruct((length, features), jnp.bfloat16),
            jax.ShapeDtypeStruct((length, 2 * rank), jnp.bfloat16),
        ),
        in_specs=[
            early(rows),
            early(length),
            early(length),
            early(rows),
            late(features),
            late(features),
            late(rank),
            late(rank),
        ],
        out_specs=(
            early(rows),
            late(length),
            late(length),
            fixed(length, features),
            fixed(length, 2 * rank),
        ),
        scratch_shapes=[buffer] * 5
        + [
            pltpu.VMEM((length, features), jnp.float32),
            pltpu.VMEM((length, rank), jnp.float32),
            pltpu.VMEM((length, rank), jnp.float32),
        ]
        + [semaphores] * 4,
        compiler_params=pltpu.CompilerParams(
            collective_id=0, has_side_effects=True, vmem_limit_bytes=50 * 1024 * 1024
        ),
        cost_estimate=pl.CostEstimate(
            flops=14 * rows * length * columns,
            bytes_accessed=12 * rows * columns,
            transcendentals=rows * length * heads,
        ),
        name="attention",
    )(queries, keys, values, grad_attention, key_weight, value_weight, key_up, value_up)


def exchange(axis, size, source, landing, send, recv):
    me = lax.axis_index(axis)

    def copy(offset):
        return pltpu.make_async_remote_copy(
            src_ref=source,
            dst_ref=landing.at[me],
            send_sem=send.at[offset],
            recv_sem=recv.at[me],
            device_id={axis: lax.rem(me + offset, size)},
            device_id_type=MESH,
        )

    def arrival(offset):
        other = lax.rem(me + offset, size)
        return pltpu.make_async_remote_copy(
            src_ref=source,
            dst_ref=landing.at[other],
            send_sem=send.at[offset],
            recv_sem=recv.at[other],
            device_id={axis: other},
            device_id_type=MESH,
        )

    def start():
        for offset in range(1, size):
            copy(offset).start()

    def finish():
        for offset in range(1, size):
            arrival(offset).wait_recv()
        for offset in range(1, size):
            copy(offset).wait_send()

    return start, finish


def tail_kernel(
    n,
    splits,
    prompts,
    slices,
    features_whole,
    context_part,
    project_part,
    normed,
    scale,
    gain,
    down,
    latent,
    key_grad,
    value_grad,
    out_weight,
    grad_text,
    grad_hidden,
    down_sum,
    up_sum,
    weight,
    grads,
    context_all,
    project_all,
    scaled,
    sum_own,
    sum_all,
    up_own,
    up_all,
    down_own,
    down_all,
    rows_own,
    rows_all,
    part,
    up_in,
    up_out,
    down_in,
    down_out,
    weight_sem,
    grads_sem,
    context_send,
    context_recv,
    project_send,
    project_recv,
    sum_send,
    sum_recv,
    up_dp_send,
    up_dp_recv,
    down_dp_send,
    down_dp_recv,
    rows_send,
    rows_recv,
    high_send,
    high_recv,
    low_send,
    low_recv,
):
    me = lax.axis_index("seq")
    split = lax.axis_index("tp")
    prompt = lax.axis_index("dp")
    length = grad_text.shape[0]
    width = part.shape[3]
    block = part.shape[2]
    lag = n
    has_low = me > 0
    has_high = me < n - 1

    key_fetch = pltpu.make_async_copy(key_grad, grads, grads_sem)
    value_fetch = pltpu.make_async_copy(value_grad, grads, grads_sem)
    weight_fetch = pltpu.make_async_copy(out_weight, weight, weight_sem)

    @pl.when(me < n // 2)
    def _():
        key_fetch.start()

    @pl.when(me >= n // 2)
    def _():
        value_fetch.start()

    weight_fetch.start()

    barrier = pltpu.get_barrier_semaphore()
    for axis, size in (("tp", splits), ("seq", n), ("dp", prompts)):
        for offset in range(1, size):
            pl.semaphore_signal(
                barrier,
                inc=1,
                device_id={axis: lax.rem(lax.axis_index(axis) + offset, size)},
                device_id_type=MESH,
            )
    pl.semaphore_wait(barrier, splits + n + prompts - 3)

    project_start, project_finish = exchange(
        "tp", splits, project_part, project_all, project_send, project_recv
    )
    context_start, context_finish = exchange(
        "tp", splits, context_part, context_all, context_send, context_recv
    )
    sum_start, sum_finish = exchange("seq", n, sum_own, sum_all, sum_send, sum_recv)
    up_start, up_finish = exchange("dp", prompts, up_own, up_all, up_dp_send, up_dp_recv)
    down_start, down_finish = exchange(
        "dp", prompts, down_own, down_all, down_dp_send, down_dp_recv
    )
    rows_start, rows_finish = exchange("seq", n, rows_own, rows_all, rows_send, rows_recv)

    project_start()
    context_start()
    project_all[split] = project_part[...]
    context_all[split] = context_part[...]
    key_fetch.wait()
    up_own[...] = dot(latent[...], grads[...], 1, 0).astype(jnp.bfloat16)
    up_all[prompt] = up_own[...]
    up_start()

    project_finish()
    back = project_all[0].astype(jnp.float32)
    for index in range(1, splits):
        back = back + project_all[index].astype(jnp.float32)
    back = back.astype(jnp.bfloat16)
    low_rank = dot(back, down[...], 1, 1)
    context_finish()
    whole = context_all[0].astype(jnp.float32)
    for index in range(1, splits):
        whole = whole + context_all[index].astype(jnp.float32)
    scaled[...] = gain[...] * (whole + low_rank)
    local_sum = jnp.sum(normed[...].astype(jnp.float32) * scaled[...], axis=1, keepdims=True)
    sum_own[...] = jnp.transpose(jnp.broadcast_to(local_sum, (length, 128)))[:8, :]
    sum_all[me] = sum_own[...]
    sum_start()

    context = (normed[...].astype(jnp.float32) * gain[...]).astype(jnp.bfloat16)
    down_own[...] = dot(back, context, 0, 0).astype(jnp.bfloat16)
    down_all[prompt] = down_own[...]
    down_start()
    weight_fetch.wait()

    sum_finish()
    token_sum = sum_all[0]
    for index in range(1, n):
        token_sum = token_sum + sum_all[index]
    token_column = jnp.transpose(jnp.broadcast_to(token_sum[:1, :], (128, length)))[:, :1]
    grad_text[...] = (
        scale[...]
        * (scaled[...] - normed[...].astype(jnp.float32) * (token_column / features_whole))
    ).astype(jnp.bfloat16)

    def high_copy(chunk, owner, source):
        return pltpu.make_async_remote_copy(
            src_ref=source.at[chunk, owner],
            dst_ref=up_in.at[chunk, owner],
            send_sem=high_send.at[chunk, owner],
            recv_sem=high_recv.at[chunk, owner],
            device_id={"seq": lax.rem(me + 1, n)},
            device_id_type=MESH,
        )

    def low_copy(chunk, owner, source):
        return pltpu.make_async_remote_copy(
            src_ref=source.at[chunk, owner],
            dst_ref=down_in.at[chunk, owner],
            send_sem=low_send.at[chunk, owner],
            recv_sem=low_recv.at[chunk, owner],
            device_id={"seq": lax.rem(me + n - 1, n)},
            device_id_type=MESH,
        )

    def hidden_step(step, carry):
        @pl.when(step < slices)
        def _():
            slab = weight[pl.ds(pl.multiple_of(step * width, width), width), :]
            product = dot(grad_text[...], slab, 1, 1).astype(jnp.bfloat16)
            part[step] = product.reshape(n, block, width)

        high = step - me
        high_live = jnp.logical_and(high >= 0, high < slices)

        @pl.when(jnp.logical_and(high_live, me == 0))
        def _():
            def send(index, carry):
                high_copy(high, n - 1 - index, part).start()
                return carry

            lax.fori_loop(0, n - 1, send, 0)
            up_in[high, 0] = jnp.zeros(up_in.shape[2:], up_in.dtype)

        @pl.when(jnp.logical_and(high_live, has_low))
        def _():
            def forward(index, carry):
                owner = n - 1 - index
                high_copy(high, owner, up_out).wait_recv()
                up_out[high, owner] = up_in[high, owner] + part[high, owner]
                high_copy(high, owner, up_out).start()
                return carry

            lax.fori_loop(0, n - 1 - me, forward, 0)
            high_copy(high, me, up_out).wait_recv()

        low = step - (n - 1 - me)
        low_live = jnp.logical_and(low >= 0, low < slices)

        @pl.when(jnp.logical_and(low_live, me == n - 1))
        def _():
            def send(owner, carry):
                low_copy(low, owner, part).start()
                return carry

            lax.fori_loop(0, n - 1, send, 0)
            down_in[low, n - 1] = jnp.zeros(down_in.shape[2:], down_in.dtype)

        @pl.when(jnp.logical_and(low_live, has_high))
        def _():
            def forward(owner, carry):
                low_copy(low, owner, down_out).wait_recv()
                down_out[low, owner] = down_in[low, owner] + part[low, owner]
                low_copy(low, owner, down_out).start()
                return carry

            lax.fori_loop(0, me, forward, 0)
            low_copy(low, me, down_out).wait_recv()

        @pl.when(step >= lag)
        def _():
            chunk = step - lag

            def high_done(owner, carry):
                high_copy(chunk, owner, up_out).wait_send()
                return carry

            def low_done(owner, carry):
                low_copy(chunk, owner, down_out).wait_send()
                return carry

            lax.fori_loop(me + 1, n, high_done, 0)
            lax.fori_loop(0, me, low_done, 0)
            grad_hidden[:, pl.ds(pl.multiple_of(chunk * width, width), width)] = (
                up_in[chunk, me].astype(jnp.float32)
                + part[chunk, me].astype(jnp.float32)
                + down_in[chunk, me].astype(jnp.float32)
            ).astype(jnp.bfloat16)

        return carry

    lax.fori_loop(0, slices // 2, hidden_step, 0)

    up_finish()
    up_total = up_all[0].astype(jnp.float32)
    for index in range(1, prompts):
        up_total = up_total + up_all[index].astype(jnp.float32)
    rows_own[...] = (up_total / prompts).astype(jnp.bfloat16)
    rows_all[me] = rows_own[...]
    rows_start()
    down_finish()
    down_total = down_all[0].astype(jnp.float32)
    for index in range(1, prompts):
        down_total = down_total + down_all[index].astype(jnp.float32)
    down_sum[...] = down_total / prompts

    lax.fori_loop(slices // 2, slices + lag, hidden_step, 0)
    rows_finish()
    up_sum[...] = rows_all[...].astype(jnp.float32)


def tail(
    context_part,
    project_part,
    normed,
    scale,
    gain,
    down,
    latent,
    key_grad,
    value_grad,
    out_weight,
):
    length, features = context_part.shape
    pair = project_part.shape[1]
    columns = key_grad.shape[1]
    hidden = out_weight.shape[0]
    n, splits, prompts = lax.axis_size("seq"), lax.axis_size("tp"), lax.axis_size("dp")
    width = 512 if hidden % 512 == 0 else 256
    slices = hidden // width
    block = length // n
    share = pair // n
    low = jnp.bfloat16
    buffer = pltpu.VMEM((slices, n, block, width), low)
    dma = pltpu.SemaphoreType.DMA
    vmem = pl.BlockSpec(memory_space=pltpu.VMEM)
    hbm = pl.BlockSpec(memory_space=pl.ANY)
    return pl.pallas_call(
        functools.partial(tail_kernel, n, splits, prompts, slices, features * n),
        out_shape=(
            jax.ShapeDtypeStruct((length, features), low),
            jax.ShapeDtypeStruct((block, hidden), low),
            jax.ShapeDtypeStruct((pair, features), jnp.float32),
            jax.ShapeDtypeStruct((n, share, columns), jnp.float32),
        ),
        in_specs=[vmem] * 7 + [hbm] * 3,
        out_specs=(vmem,) * 4,
        scratch_shapes=[
            pltpu.VMEM(out_weight.shape, low),
            pltpu.VMEM(key_grad.shape, low),
            pltpu.VMEM((splits, length, features), low),
            pltpu.VMEM((splits, length, pair), low),
            pltpu.VMEM((length, features), jnp.float32),
            pltpu.VMEM((8, length), jnp.float32),
            pltpu.VMEM((n, 8, length), jnp.float32),
            pltpu.VMEM((share, columns), low),
            pltpu.VMEM((prompts, share, columns), low),
            pltpu.VMEM((pair, features), low),
            pltpu.VMEM((prompts, pair, features), low),
            pltpu.VMEM((share, columns), low),
            pltpu.VMEM((n, share, columns), low),
        ]
        + [buffer] * 5
        + [dma, dma]
        + [dma((splits,))] * 4
        + [dma((n,))] * 2
        + [dma((prompts,))] * 4
        + [dma((n,))] * 2
        + [dma((slices, n))] * 4,
        compiler_params=pltpu.CompilerParams(
            collective_id=1, has_side_effects=True, vmem_limit_bytes=60 * 1024 * 1024
        ),
        name="tail",
    )(
        context_part,
        project_part,
        normed,
        scale,
        gain,
        down,
        latent,
        key_grad,
        value_grad,
        out_weight,
    )


def shards(
    queries,
    keys,
    values,
    grad_attention,
    normed,
    norm_scale,
    norm_gain,
    key_weight,
    value_weight,
    key_down,
    key_up,
    value_down,
    value_up,
    out_weight,
):
    context = (normed[0].astype(jnp.float32) * norm_gain).astype(jnp.bfloat16)
    latent_part = jnp.concatenate(
        [
            jnp.dot(context, key_down, preferred_element_type=jnp.float32),
            jnp.dot(context, value_down, preferred_element_type=jnp.float32),
        ],
        axis=1,
    )
    latent = lax.psum(latent_part.astype(jnp.bfloat16), "seq")
    n = lax.axis_size("seq")
    rank = key_down.shape[1]
    share = 2 * rank // n
    grad_query, key_grad, value_grad, context_part, project_part = attention_grads(
        queries[0],
        keys[0],
        values[0],
        grad_attention[0],
        key_weight,
        value_weight,
        key_up,
        value_up,
    )
    latent_rows = lax.dynamic_slice_in_dim(latent.T, lax.axis_index("seq") * share, share, 0)
    grad_text, grad_hidden, down_sum, up_sum = tail(
        context_part,
        project_part,
        normed[0],
        norm_scale[0][:, None],
        norm_gain[None, :],
        jnp.concatenate([key_down, value_down], axis=1),
        latent_rows,
        key_grad,
        value_grad,
        out_weight,
    )
    up_rows = up_sum.reshape(2 * rank, up_sum.shape[2])
    return (
        grad_query[None],
        grad_text[None],
        grad_hidden[None],
        down_sum[:rank].T,
        up_rows[:rank],
        down_sum[rank:].T,
        up_rows[rank:],
    )


def solution(mesh):
    return jax.shard_map(
        shards,
        mesh=mesh,
        in_specs=(
            P("dp", "seq", "tp"),
            P("dp", None, "tp"),
            P("dp", None, "tp"),
            P("dp", "seq", "tp"),
            P("dp", None, "seq"),
            P("dp", None),
            P("seq"),
            P("seq", "tp"),
            P("seq", "tp"),
            P("seq", None),
            P(None, "tp"),
            P("seq", None),
            P(None, "tp"),
            P("tp", "seq"),
        ),
        out_specs=(
            P("dp", "seq", "tp"),
            P("dp", None, "seq"),
            P("dp", "seq", "tp"),
            P("seq", None),
            P(None, "tp"),
            P("seq", None),
            P(None, "tp"),
        ),
        check_vma=False,
    )
```

```python
import functools

import jax
import jax.numpy as jnp
from jax import lax
from jax.experimental import pallas as pl
from jax.experimental.pallas import tpu as pltpu
from jax.sharding import PartitionSpec as P

HD = 128
MESH = pl.DeviceIdType.MESH


def dot(left_side, right_side, left_dim, right_dim):
    return lax.dot_general(
        left_side,
        right_side,
        (((left_dim,), (right_dim,)), ((), ())),
        preferred_element_type=jnp.float32,
    )


def attention_kernel(
    n,
    heads,
    lag,
    queries,
    keys,
    values,
    grads,
    key_weight,
    value_weight,
    key_up,
    value_up,
    grad_query,
    key_grad,
    value_grad,
    context,
    project,
    part,
    up_in,
    up_out,
    down_in,
    down_out,
    total,
    key_total,
    value_total,
    up_send,
    up_recv,
    down_send,
    down_recv,
):
    step = pl.program_id(0)
    me = lax.axis_index("seq")
    factor = HD ** (-0.5)
    has_low = me > 0
    has_high = me < n - 1

    def up_copy(chunk, half, source):
        return pltpu.make_async_remote_copy(
            src_ref=source.at[chunk, half],
            dst_ref=up_in.at[chunk, half],
            send_sem=up_send.at[chunk, half],
            recv_sem=up_recv.at[chunk, half],
            device_id={"seq": lax.rem(me + 1, n)},
            device_id_type=MESH,
        )

    def down_copy(chunk, half, source):
        return pltpu.make_async_remote_copy(
            src_ref=source.at[chunk, half],
            dst_ref=down_in.at[chunk, half],
            send_sem=down_send.at[chunk, half],
            recv_sem=down_recv.at[chunk, half],
            device_id={"seq": lax.rem(me + n - 1, n)},
            device_id_type=MESH,
        )

    @pl.when(step == 0)
    def _():
        barrier = pltpu.get_barrier_semaphore()

        @pl.when(has_low)
        def _():
            pl.semaphore_signal(
                barrier,
                inc=1,
                device_id={"seq": lax.rem(me + n - 1, n)},
                device_id_type=MESH,
            )

        @pl.when(has_high)
        def _():
            pl.semaphore_signal(
                barrier, inc=1, device_id={"seq": lax.rem(me + 1, n)}, device_id_type=MESH
            )

        total[...] = jnp.zeros_like(total)
        key_total[...] = jnp.zeros_like(key_total)
        value_total[...] = jnp.zeros_like(value_total)

        pl.semaphore_wait(barrier, has_low.astype(jnp.int32) + has_high.astype(jnp.int32))

    @pl.when(step < heads)
    def _():
        query, key, value, grad = queries[...], keys[...], values[...], grads[...]
        scores = dot(key, query, 1, 1) * factor
        weights = jnp.exp(scores - jnp.max(scores, axis=0, keepdims=True))
        probability = weights * (1.0 / jnp.sum(weights, axis=0, keepdims=True))
        part[step, 1] = dot(probability.astype(jnp.bfloat16), grad, 1, 0).astype(jnp.bfloat16)
        grad_probs = dot(value, grad, 1, 1)
        grad_scores = probability * (
            grad_probs - jnp.sum(probability * grad_probs, axis=0, keepdims=True)
        )
        grad_low = grad_scores.astype(jnp.bfloat16)
        part[step, 0] = (dot(grad_low, query, 1, 0) * factor).astype(jnp.bfloat16)
        grad_query[...] = (dot(grad_low, key, 0, 0) * factor).astype(jnp.bfloat16)

    up_chunk = step - me
    up_live = jnp.logical_and(up_chunk >= 0, up_chunk < heads)
    down_chunk = step - (n - 1 - me)
    down_live = jnp.logical_and(down_chunk >= 0, down_chunk < heads)

    @pl.when(jnp.logical_and(up_live, me == 0))
    def _():
        for half in (1, 0):
            up_copy(up_chunk, half, part).start()
        up_in[up_chunk] = jnp.zeros(up_in.shape[1:], up_in.dtype)

    @pl.when(jnp.logical_and(down_live, me == n - 1))
    def _():
        for half in (1, 0):
            down_copy(down_chunk, half, part).start()
        down_in[down_chunk] = jnp.zeros(down_in.shape[1:], down_in.dtype)

    for half in (1, 0):

        @pl.when(jnp.logical_and(up_live, has_low))
        def _():
            up_copy(up_chunk, half, up_out).wait_recv()

            @pl.when(has_high)
            def _():
                up_out[up_chunk, half] = up_in[up_chunk, half] + part[up_chunk, half]
                up_copy(up_chunk, half, up_out).start()

        @pl.when(jnp.logical_and(down_live, has_high))
        def _():
            down_copy(down_chunk, half, down_out).wait_recv()

            @pl.when(has_low)
            def _():
                down_out[down_chunk, half] = down_in[down_chunk, half] + part[down_chunk, half]
                down_copy(down_chunk, half, down_out).start()

    @pl.when(step >= lag)
    def _():
        chunk = step - lag

        @pl.when(has_high)
        def _():
            for half in (1, 0):
                up_copy(chunk, half, up_out).wait_send()

        @pl.when(has_low)
        def _():
            for half in (1, 0):
                down_copy(chunk, half, down_out).wait_send()

        both = (
            up_in[chunk].astype(jnp.float32)
            + part[chunk].astype(jnp.float32)
            + down_in[chunk].astype(jnp.float32)
        ).astype(jnp.bfloat16)
        key_grad[...] = both[0]
        value_grad[...] = both[1]
        slab = jnp.concatenate([key_weight[...], value_weight[...]], axis=1)
        total[...] += dot(jnp.concatenate([both[0], both[1]], axis=1), slab, 1, 1)
        key_total[...] += dot(both[0], key_up[...], 1, 1)
        value_total[...] += dot(both[1], value_up[...], 1, 1)

    @pl.when(step == heads + lag - 1)
    def _():
        context[...] = total[...].astype(jnp.bfloat16)
        project[...] = jnp.concatenate([key_total[...], value_total[...]], axis=1).astype(
            jnp.bfloat16
        )


def attention_grads(
    queries, keys, values, grad_attention, key_weight, value_weight, key_up, value_up
):
    rows, columns = queries.shape
    length = keys.shape[0]
    features = key_weight.shape[0]
    rank = key_up.shape[0]
    heads = columns // HD
    n = lax.axis_size("seq")
    lag = n + 1

    def early(height):
        return pl.BlockSpec((height, HD), lambda step: (0, jnp.minimum(step, heads - 1)))

    def late(height):
        return pl.BlockSpec((height, HD), lambda step: (0, jnp.maximum(step - lag, 0)))

    def fixed(height, width):
        return pl.BlockSpec((height, width), lambda step: (0, 0))

    buffer = pltpu.VMEM((heads, 2, length, HD), jnp.bfloat16)
    semaphores = pltpu.SemaphoreType.DMA((heads, 2))
    return pl.pallas_call(
        functools.partial(attention_kernel, n, heads, lag),
        grid=(heads + lag,),
        out_shape=(
            jax.ShapeDtypeStruct((rows, columns), jnp.bfloat16),
            jax.ShapeDtypeStruct((length, columns), jnp.bfloat16),
            jax.ShapeDtypeStruct((length, columns), jnp.bfloat16),
            jax.ShapeDtypeStruct((length, features), jnp.bfloat16),
            jax.ShapeDtypeStruct((length, 2 * rank), jnp.bfloat16),
        ),
        in_specs=[
            early(rows),
            early(length),
            early(length),
            early(rows),
            late(features),
            late(features),
            late(rank),
            late(rank),
        ],
        out_specs=(
            early(rows),
            late(length),
            late(length),
            fixed(length, features),
            fixed(length, 2 * rank),
        ),
        scratch_shapes=[buffer] * 5
        + [
            pltpu.VMEM((length, features), jnp.float32),
            pltpu.VMEM((length, rank), jnp.float32),
            pltpu.VMEM((length, rank), jnp.float32),
        ]
        + [semaphores] * 4,
        compiler_params=pltpu.CompilerParams(
            collective_id=0, has_side_effects=True, vmem_limit_bytes=50 * 1024 * 1024
        ),
        cost_estimate=pl.CostEstimate(
            flops=14 * rows * length * columns,
            bytes_accessed=12 * rows * columns,
            transcendentals=rows * length * heads,
        ),
        name="attention",
    )(queries, keys, values, grad_attention, key_weight, value_weight, key_up, value_up)


def exchange(axis, size, source, landing, send, recv):
    me = lax.axis_index(axis)

    def copy(offset):
        return pltpu.make_async_remote_copy(
            src_ref=source,
            dst_ref=landing.at[me],
            send_sem=send.at[offset],
            recv_sem=recv.at[me],
            device_id={axis: lax.rem(me + offset, size)},
            device_id_type=MESH,
        )

    def arrival(offset):
        other = lax.rem(me + offset, size)
        return pltpu.make_async_remote_copy(
            src_ref=source,
            dst_ref=landing.at[other],
            send_sem=send.at[offset],
            recv_sem=recv.at[other],
            device_id={axis: other},
            device_id_type=MESH,
        )

    def start():
        for offset in range(1, size):
            copy(offset).start()

    def finish():
        for offset in range(1, size):
            arrival(offset).wait_recv()
        for offset in range(1, size):
            copy(offset).wait_send()

    return start, finish


def tail_kernel(
    n,
    splits,
    prompts,
    slices,
    features_whole,
    context_part,
    project_part,
    normed,
    scale,
    gain,
    key_down,
    value_down,
    key_grad,
    value_grad,
    out_weight,
    grad_text,
    grad_hidden,
    key_down_grad,
    value_down_grad,
    key_up_grad,
    value_up_grad,
    weight,
    grads,
    context_all,
    project_all,
    scaled,
    sum_own,
    sum_all,
    up_own,
    up_all,
    down_own,
    down_all,
    rows_own,
    rows_all,
    latent_own,
    latent_all,
    part,
    up_in,
    up_out,
    down_in,
    down_out,
    weight_sem,
    grads_sem,
    context_send,
    context_recv,
    project_send,
    project_recv,
    sum_send,
    sum_recv,
    up_dp_send,
    up_dp_recv,
    down_dp_send,
    down_dp_recv,
    rows_send,
    rows_recv,
    latent_send,
    latent_recv,
    high_send,
    high_recv,
    low_send,
    low_recv,
):
    me = lax.axis_index("seq")
    split = lax.axis_index("tp")
    prompt = lax.axis_index("dp")
    length = grad_text.shape[0]
    width = part.shape[3]
    block = part.shape[2]
    lag = n
    has_low = me > 0
    has_high = me < n - 1

    key_fetch = pltpu.make_async_copy(key_grad, grads, grads_sem)
    value_fetch = pltpu.make_async_copy(value_grad, grads, grads_sem)
    weight_fetch = pltpu.make_async_copy(out_weight, weight, weight_sem)

    @pl.when(me < n // 2)
    def _():
        key_fetch.start()

    @pl.when(me >= n // 2)
    def _():
        value_fetch.start()

    weight_fetch.start()

    barrier = pltpu.get_barrier_semaphore()
    for axis, size in (("tp", splits), ("seq", n), ("dp", prompts)):
        for offset in range(1, size):
            pl.semaphore_signal(
                barrier,
                inc=1,
                device_id={axis: lax.rem(lax.axis_index(axis) + offset, size)},
                device_id_type=MESH,
            )
    pl.semaphore_wait(barrier, splits + n + prompts - 3)

    project_start, project_finish = exchange(
        "tp", splits, project_part, project_all, project_send, project_recv
    )
    context_start, context_finish = exchange(
        "tp", splits, context_part, context_all, context_send, context_recv
    )
    sum_start, sum_finish = exchange("seq", n, sum_own, sum_all, sum_send, sum_recv)
    up_start, up_finish = exchange("dp", prompts, up_own, up_all, up_dp_send, up_dp_recv)
    down_start, down_finish = exchange(
        "dp", prompts, down_own, down_all, down_dp_send, down_dp_recv
    )
    rows_start, rows_finish = exchange("seq", n, rows_own, rows_all, rows_send, rows_recv)

    def latent_copy(offset):
        other = lax.rem(me + offset, n)
        return pltpu.make_async_remote_copy(
            src_ref=latent_own.at[other],
            dst_ref=latent_all.at[me],
            send_sem=latent_send.at[offset],
            recv_sem=latent_recv.at[me],
            device_id={"seq": other},
            device_id_type=MESH,
        )

    def latent_arrival(offset):
        other = lax.rem(me + offset, n)
        return pltpu.make_async_remote_copy(
            src_ref=latent_own.at[other],
            dst_ref=latent_all.at[other],
            send_sem=latent_send.at[offset],
            recv_sem=latent_recv.at[other],
            device_id={"seq": other},
            device_id_type=MESH,
        )

    project_start()
    context_start()
    project_all[split] = project_part[...]
    context_all[split] = context_part[...]
    context = (normed[...].astype(jnp.float32) * gain[...]).astype(jnp.bfloat16)
    latent_rows = jnp.concatenate(
        [dot(key_down[...], context, 0, 1), dot(value_down[...], context, 0, 1)], axis=0
    )
    latent_own[...] = latent_rows.reshape(latent_own.shape).astype(jnp.bfloat16)
    for offset in range(1, n):
        latent_copy(offset).start()
    latent_all[me] = latent_own[me]

    project_finish()
    back = project_all[0].astype(jnp.float32)
    for index in range(1, splits):
        back = back + project_all[index].astype(jnp.float32)
    back = back.astype(jnp.bfloat16)
    rank = key_down.shape[1]
    low_rank = dot(back[:, :rank], key_down[...], 1, 1) + dot(
        back[:, rank:], value_down[...], 1, 1
    )
    context_finish()
    whole = context_all[0].astype(jnp.float32)
    for index in range(1, splits):
        whole = whole + context_all[index].astype(jnp.float32)
    scaled[...] = gain[...] * (whole + low_rank)
    local_sum = jnp.sum(normed[...].astype(jnp.float32) * scaled[...], axis=1, keepdims=True)
    sum_own[...] = jnp.transpose(jnp.broadcast_to(local_sum, (length, 128)))[:8, :]
    sum_all[me] = sum_own[...]
    sum_start()

    down_own[...] = dot(back, context, 0, 0).astype(jnp.bfloat16)
    down_all[prompt] = down_own[...]
    down_start()
    for offset in range(1, n):
        latent_arrival(offset).wait_recv()
    latent = latent_all[0].astype(jnp.float32)
    for index in range(1, n):
        latent = latent + latent_all[index].astype(jnp.float32)
    key_fetch.wait()
    up_own[...] = dot(latent.astype(jnp.bfloat16), grads[...], 1, 0).astype(jnp.bfloat16)
    up_all[prompt] = up_own[...]
    up_start()
    weight_fetch.wait()
    for offset in range(1, n):
        latent_copy(offset).wait_send()

    sum_finish()
    token_sum = sum_all[0]
    for index in range(1, n):
        token_sum = token_sum + sum_all[index]
    token_column = jnp.transpose(jnp.broadcast_to(token_sum[:1, :], (128, length)))[:, :1]
    grad_text[...] = (
        scale[...]
        * (scaled[...] - normed[...].astype(jnp.float32) * (token_column / features_whole))
    ).astype(jnp.bfloat16)

    def high_copy(chunk, owner, source):
        return pltpu.make_async_remote_copy(
            src_ref=source.at[chunk, owner],
            dst_ref=up_in.at[chunk, owner],
            send_sem=high_send.at[chunk, owner],
            recv_sem=high_recv.at[chunk, owner],
            device_id={"seq": lax.rem(me + 1, n)},
            device_id_type=MESH,
        )

    def low_copy(chunk, owner, source):
        return pltpu.make_async_remote_copy(
            src_ref=source.at[chunk, owner],
            dst_ref=down_in.at[chunk, owner],
            send_sem=low_send.at[chunk, owner],
            recv_sem=low_recv.at[chunk, owner],
            device_id={"seq": lax.rem(me + n - 1, n)},
            device_id_type=MESH,
        )

    def hidden_step(step, carry):
        @pl.when(step < slices)
        def _():
            slab = weight[pl.ds(pl.multiple_of(step * width, width), width), :]
            product = dot(grad_text[...], slab, 1, 1).astype(jnp.bfloat16)
            part[step] = product.reshape(n, block, width)

        high = step - me
        high_live = jnp.logical_and(high >= 0, high < slices)

        @pl.when(jnp.logical_and(high_live, me == 0))
        def _():
            def send(index, carry):
                high_copy(high, n - 1 - index, part).start()
                return carry

            lax.fori_loop(0, n - 1, send, 0)
            up_in[high, 0] = jnp.zeros(up_in.shape[2:], up_in.dtype)

        @pl.when(jnp.logical_and(high_live, has_low))
        def _():
            def forward(index, carry):
                owner = n - 1 - index
                high_copy(high, owner, up_out).wait_recv()
                up_out[high, owner] = up_in[high, owner] + part[high, owner]
                high_copy(high, owner, up_out).start()
                return carry

            lax.fori_loop(0, n - 1 - me, forward, 0)
            high_copy(high, me, up_out).wait_recv()

        low = step - (n - 1 - me)
        low_live = jnp.logical_and(low >= 0, low < slices)

        @pl.when(jnp.logical_and(low_live, me == n - 1))
        def _():
            def send(owner, carry):
                low_copy(low, owner, part).start()
                return carry

            lax.fori_loop(0, n - 1, send, 0)
            down_in[low, n - 1] = jnp.zeros(down_in.shape[2:], down_in.dtype)

        @pl.when(jnp.logical_and(low_live, has_high))
        def _():
            def forward(owner, carry):
                low_copy(low, owner, down_out).wait_recv()
                down_out[low, owner] = down_in[low, owner] + part[low, owner]
                low_copy(low, owner, down_out).start()
                return carry

            lax.fori_loop(0, me, forward, 0)
            low_copy(low, me, down_out).wait_recv()

        @pl.when(step >= lag)
        def _():
            chunk = step - lag

            def high_done(owner, carry):
                high_copy(chunk, owner, up_out).wait_send()
                return carry

            def low_done(owner, carry):
                low_copy(chunk, owner, down_out).wait_send()
                return carry

            lax.fori_loop(me + 1, n, high_done, 0)
            lax.fori_loop(0, me, low_done, 0)
            grad_hidden[:, pl.ds(pl.multiple_of(chunk * width, width), width)] = (
                up_in[chunk, me].astype(jnp.float32)
                + part[chunk, me].astype(jnp.float32)
                + down_in[chunk, me].astype(jnp.float32)
            ).astype(jnp.bfloat16)

        return carry

    lax.fori_loop(0, slices // 2, hidden_step, 0)

    up_finish()
    up_total = up_all[0].astype(jnp.float32)
    for index in range(1, prompts):
        up_total = up_total + up_all[index].astype(jnp.float32)
    rows_own[...] = (up_total / prompts).astype(jnp.bfloat16)
    rows_all[me] = rows_own[...]
    rows_start()
    down_finish()
    down_total = down_all[0].astype(jnp.float32)
    for index in range(1, prompts):
        down_total = down_total + down_all[index].astype(jnp.float32)
    key_down_grad[...] = down_total[:rank] / prompts
    value_down_grad[...] = down_total[rank:] / prompts

    lax.fori_loop(slices // 2, slices + lag, hidden_step, 0)
    rows_finish()
    key_up_grad[...] = rows_all[: n // 2].astype(jnp.float32).reshape(key_up_grad.shape)
    value_up_grad[...] = rows_all[n // 2 :].astype(jnp.float32).reshape(value_up_grad.shape)


def tail(
    context_part,
    project_part,
    normed,
    scale,
    gain,
    key_down,
    value_down,
    key_grad,
    value_grad,
    out_weight,
):
    length, features = context_part.shape
    pair = project_part.shape[1]
    columns = key_grad.shape[1]
    hidden = out_weight.shape[0]
    n, splits, prompts = lax.axis_size("seq"), lax.axis_size("tp"), lax.axis_size("dp")
    width = 512 if hidden % 512 == 0 else 256
    slices = hidden // width
    block = length // n
    share = pair // n
    low = jnp.bfloat16
    buffer = pltpu.VMEM((slices, n, block, width), low)
    dma = pltpu.SemaphoreType.DMA
    vmem = pl.BlockSpec(memory_space=pltpu.VMEM)
    hbm = pl.BlockSpec(memory_space=pl.ANY)
    return pl.pallas_call(
        functools.partial(tail_kernel, n, splits, prompts, slices, features * n),
        out_shape=(
            jax.ShapeDtypeStruct((length, features), low),
            jax.ShapeDtypeStruct((block, hidden), low),
            jax.ShapeDtypeStruct((pair // 2, features), jnp.float32),
            jax.ShapeDtypeStruct((pair // 2, features), jnp.float32),
            jax.ShapeDtypeStruct((pair // 2, columns), jnp.float32),
            jax.ShapeDtypeStruct((pair // 2, columns), jnp.float32),
        ),
        in_specs=[vmem] * 7 + [hbm] * 3,
        out_specs=(vmem,) * 6,
        scratch_shapes=[
            pltpu.VMEM(out_weight.shape, low),
            pltpu.VMEM(key_grad.shape, low),
            pltpu.VMEM((splits, length, features), low),
            pltpu.VMEM((splits, length, pair), low),
            pltpu.VMEM((length, features), jnp.float32),
            pltpu.VMEM((8, length), jnp.float32),
            pltpu.VMEM((n, 8, length), jnp.float32),
            pltpu.VMEM((share, columns), low),
            pltpu.VMEM((prompts, share, columns), low),
            pltpu.VMEM((pair, features), low),
            pltpu.VMEM((prompts, pair, features), low),
            pltpu.VMEM((share, columns), low),
            pltpu.VMEM((n, share, columns), low),
            pltpu.VMEM((n, share, length), low),
            pltpu.VMEM((n, share, length), low),
        ]
        + [buffer] * 5
        + [dma, dma]
        + [dma((splits,))] * 4
        + [dma((n,))] * 2
        + [dma((prompts,))] * 4
        + [dma((n,))] * 4
        + [dma((slices, n))] * 4,
        compiler_params=pltpu.CompilerParams(
            collective_id=1, has_side_effects=True, vmem_limit_bytes=60 * 1024 * 1024
        ),
        name="tail",
    )(
        context_part,
        project_part,
        normed,
        scale,
        gain,
        key_down,
        value_down,
        key_grad,
        value_grad,
        out_weight,
    )


def shards(
    queries,
    keys,
    values,
    grad_attention,
    normed,
    norm_scale,
    norm_gain,
    key_weight,
    value_weight,
    key_down,
    key_up,
    value_down,
    value_up,
    out_weight,
):
    grad_query, key_grad, value_grad, context_part, project_part = attention_grads(
        queries[0],
        keys[0],
        values[0],
        grad_attention[0],
        key_weight,
        value_weight,
        key_up,
        value_up,
    )
    grad_text, grad_hidden, down_key, down_value, up_key, up_value = tail(
        context_part,
        project_part,
        normed[0],
        norm_scale[0][:, None],
        norm_gain[None, :],
        key_down,
        value_down,
        key_grad,
        value_grad,
        out_weight,
    )
    return (
        grad_query[None],
        grad_text[None],
        grad_hidden[None],
        down_key.T,
        up_key,
        down_value.T,
        up_value,
    )


def solution(mesh):
    return jax.shard_map(
        shards,
        mesh=mesh,
        in_specs=(
            P("dp", "seq", "tp"),
            P("dp", None, "tp"),
            P("dp", None, "tp"),
            P("dp", "seq", "tp"),
            P("dp", None, "seq"),
            P("dp", None),
            P("seq"),
            P("seq", "tp"),
            P("seq", "tp"),
            P("seq", None),
            P(None, "tp"),
            P("seq", None),
            P(None, "tp"),
            P("tp", "seq"),
        ),
        out_specs=(
            P("dp", "seq", "tp"),
            P("dp", None, "seq"),
            P("dp", "seq", "tp"),
            P("seq", None),
            P(None, "tp"),
            P("seq", None),
            P(None, "tp"),
        ),
        check_vma=False,
    )
```
